32 devices in a mesh: section: 4 (over z), row: 2 (over x), col: 4 (over y, core).
Axes of the slice: x: 2, y: 2, z: 4, core: 2. Of those that a mesh axis runs over, the one named last changes fastest.
Arguments:
- input_fwd: bfloat16 [4, 256, 2560], P('section', 'col', 'row'), may hold values from -6 to 6
- input_bwd: bfloat16 [4, 256, 2560], P('section', 'col', 'row'), may hold values from -6 to 6
- cotangent: bfloat16 [4, 256, 2560], P('section', 'col', 'row'), may hold values from -0.375 to 0.375
- shared_up: bfloat16 [2560, 16384], P('row', ('col', 'section')), may hold values from -0.125 to 0.125
- shared_down: bfloat16 [16384, 2560], P(('col', 'section'), 'row'), may hold values from -0.046875 to 0.046875
- up_left: bfloat16 [4, 2560, 256], P('section', 'row'), may hold values from -0.125 to 0.125
- up_right: bfloat16 [4, 256, 16384], P('section', None, 'col'), may hold values from -0.1875 to 0.1875
- down_left: bfloat16 [4, 16384, 256], P('section', 'col'), may hold values from -0.046875 to 0.046875
- down_right: bfloat16 [4, 256, 2560], P('section', None, 'row'), may hold values from -0.1875 to 0.1875
Outputs:
- handoff_fwd: bfloat16 [4, 256, 2560], P('section', 'col', 'row')
- handoff_bwd: bfloat16 [4, 256, 2560], P('section', 'col', 'row')
- grad_shared_up: bfloat16 [2560, 16384], P('row', ('col', 'section'))
- grad_shared_down: bfloat16 [16384, 2560], P(('col', 'section'), 'row')
- grad_up_left: float32 [4, 2560, 256], P('section', 'row')
- grad_up_right: float32 [4, 256, 16384], P('section', None, 'col')
- grad_down_left: float32 [4, 16384, 256], P('section', 'col')
- grad_down_right: float32 [4, 256, 2560], P('section', None, 'row')
The draws below stay inside these ranges and needn't reach their ends.
All inputs are finite; a program needn't handle non-finite values.
Results may differ from the reference program's by a relative error of at most 0.022.
Values may be sent and summed in bfloat16 or wider, within the bound.
A program may use at most 128 MiB of HBM per device.

```python
import jax
import jax.numpy as jnp
from jax import lax

D = 2560
FF = 16384
R = 256
MICRO = 256
SECTIONS = 4


def shard_levels(stream_key, shape, shards, low, largest):
    factor_of, own = 1.0, jax.random.fold_in(stream_key, 6)
    for dim, blocks in shards:
        draws = jnp.exp(jax.random.uniform(jax.random.fold_in(own, dim), (blocks,), jnp.float32, low / len(shards), largest / len(shards)))
        factor_of = factor_of * jnp.repeat(draws, shape[dim] // blocks).reshape([-1 if axis == dim else 1 for axis in range(len(shape))])
    return factor_of


def centred(key, extent, scale, bound, cuts=(), dtype=jnp.bfloat16):
    drawn = jax.random.normal(key, extent, jnp.float32) * scale
    if len(cuts) > 0:
        drawn = shard_levels(key, extent, cuts, -0.22, 0.18) * drawn
    return jnp.clip(drawn, min=-bound, max=bound).astype(dtype)


def setup_inputs(seed: int = 0) -> dict:
    keys = jax.random.split(jax.random.key(seed), 10)
    return {
        "input_fwd": centred(keys[0], (SECTIONS, MICRO, D), 1.0, 6.0, ((0, 4), (1, 4), (2, 2))),
        "input_bwd": centred(keys[1], (SECTIONS, MICRO, D), 1.0, 6.0, ((0, 4), (1, 4), (2, 2))),
        "cotangent": centred(keys[2], (SECTIONS, MICRO, D), (MICRO ** -0.5), 0.375, ((0, 4), (1, 4), (2, 2))),
        "shared_up": centred(keys[3], (D, FF), D ** -0.5, 0.125, ((0, 2), (1, 16))),
        "shared_down": centred(keys[4], (FF, D), FF ** -0.5, 0.046875, ((0, 16), (1, 2))),
        "up_left": centred(keys[5], (SECTIONS, D, R), D ** -0.5, 0.125, ((0, 4), (1, 2))),
        "up_right": centred(keys[6], (SECTIONS, R, FF), (0.5 * R ** -0.5), 0.1875, ((0, 4), (2, 4))),
        "down_left": centred(keys[7], (SECTIONS, FF, R), FF ** -0.5, 0.046875, ((0, 4), (1, 4))),
        "down_right": centred(keys[8], (SECTIONS, R, D), (0.5 * R ** -0.5), 0.1875, ((0, 4), (2, 2))),
    }


def product(left, right):
    return jnp.dot(left, right, preferred_element_type=jnp.float32)


def silu_slope(preact):
    sigma = jax.nn.sigmoid(preact)
    return sigma * (1.0 + preact * (1.0 - sigma))


def one_section(shared_up, shared_down, section_data):
    input_fwd, input_bwd, cotangent, up_left, up_right, down_left, down_right = section_data
    count_fwd = input_fwd.shape[0]
    normed = jnp.concatenate([input_fwd, input_bwd], axis=0)
    delta_in = product(normed, up_left).astype(jnp.bfloat16)
    preact = product(normed, shared_up) + product(delta_in, up_right)
    hidden = jax.nn.silu(preact).astype(jnp.bfloat16)
    delta_out = product(hidden, down_left).astype(jnp.bfloat16)
    out_fwd = input_fwd.astype(jnp.float32) + product(hidden[:count_fwd], shared_down) + product(delta_out[:count_fwd], down_right)
    out_fwd = out_fwd.astype(jnp.bfloat16)
    hidden_bwd = hidden[count_fwd:]
    normed_bwd = normed[count_fwd:]
    din_bwd = delta_in[count_fwd:]
    dout_bwd = delta_out[count_fwd:]
    grad_down_right = product(dout_bwd.T, cotangent)
    grad_dout = product(cotangent, down_right.T).astype(jnp.bfloat16)
    grad_down_left = product(hidden_bwd.T, grad_dout)
    grad_hidden = product(cotangent, shared_down.T) + product(grad_dout, down_left.T)
    grad_preact = (grad_hidden * silu_slope(preact[count_fwd:])).astype(jnp.bfloat16)
    grad_up_right = product(din_bwd.T, grad_preact)
    grad_din = product(grad_preact, up_right.T).astype(jnp.bfloat16)
    grad_up_left = product(normed_bwd.T, grad_din)
    grad_normed = product(grad_preact, shared_up.T) + product(grad_din, up_left.T)
    grad_input = (cotangent.astype(jnp.float32) + grad_normed).astype(jnp.bfloat16)
    term_up = product(normed_bwd.T, grad_preact).astype(jnp.bfloat16).astype(jnp.float32)
    term_down = product(hidden_bwd.T, cotangent).astype(jnp.bfloat16).astype(jnp.float32)
    return out_fwd, grad_input, term_up, term_down, grad_up_left, grad_up_right, grad_down_left, grad_down_right


def reference(input_fwd, input_bwd, cotangent, shared_up, shared_down, up_left, up_right, down_left, down_right):
    def advance(totals, section_data):
        out_fwd, grad_input, term_up, term_down, g_ul, g_ur, g_dl, g_dr = one_section(shared_up, shared_down, section_data)
        totals = (totals[0] + term_up, totals[1] + term_down)
        return totals, (out_fwd, grad_input, g_ul, g_ur, g_dl, g_dr)

    start_totals = (jnp.zeros((D, FF), jnp.float32), jnp.zeros((FF, D), jnp.float32))
    totals, outputs = lax.scan(advance, start_totals, (input_fwd, input_bwd, cotangent, up_left, up_right, down_left, down_right))
    out_fwd, grad_input, g_ul, g_ur, g_dl, g_dr = outputs
    handoff_fwd = jnp.roll(out_fwd, 1, axis=0)
    handoff_bwd = jnp.roll(grad_input, -1, axis=0)
    grad_shared_up = totals[0].astype(jnp.bfloat16)
    grad_shared_down = totals[1].astype(jnp.bfloat16)
    return handoff_fwd, handoff_bwd, grad_shared_up, grad_shared_down, g_ul, g_ur, g_dl, g_dr
```

```python
import jax
import jax.numpy as jnp
from jax import lax
from jax.sharding import PartitionSpec as P

F32, BF16 = jnp.float32, jnp.bfloat16


def from_behind(block, axis, distance):
    count = lax.axis_size(axis)
    return lax.ppermute(block, axis, [((i - distance) % count, i) for i in range(count)])


def row_sum(part):
    total = part.astype(F32)
    for step in range(1, lax.axis_size("row")):
        total = total + from_behind(part, "row", step).astype(F32)
    return total


def row_gather(block, axis):
    count, me = lax.axis_size("row"), lax.axis_index("row")
    wide = jnp.zeros(block.shape[:axis] + (count * block.shape[axis],) + block.shape[axis + 1 :], block.dtype)
    for step in range(count):
        piece = block if step == 0 else from_behind(block, "row", step)
        origin = (me - step) % count
        wide = lax.dynamic_update_slice_in_dim(wide, piece, origin * block.shape[axis], axis)
    return wide


def mm(spec, left, right):
    return jnp.einsum(spec, left, right, preferred_element_type=F32)


def silu_slope(preact):
    sigma = jax.nn.sigmoid(preact)
    return sigma * (1.0 + preact * (1.0 - sigma))


def local(
    input_fwd,
    input_bwd,
    cotangent,
    shared_up,
    shared_down,
    up_left,
    up_right,
    down_left,
    down_right,
):
    sections, rows = lax.axis_size("section"), lax.axis_size("row")
    section, row = lax.axis_index("section"), lax.axis_index("row")
    own, width = input_fwd.shape[1], input_fwd.shape[2]
    units = shared_up.shape[1]
    share = up_left.shape[2] // rows
    everyone = ("section", "col")
    micro = own * lax.axis_size("col")

    def own_share(block, axis):
        return lax.dynamic_slice_in_dim(block, row * share, share, axis)

    def own_section(tokens):
        return lax.dynamic_slice_in_dim(tokens, section * micro, micro, 0)

    def per_section(tokens):
        return tokens.reshape(sections, micro, tokens.shape[-1])

    x_fwd, x_bwd, cot = input_fwd[0], input_bwd[0], cotangent[0]
    all_bwd = lax.all_gather(x_bwd, everyone, axis=0, tiled=True)
    all_cot = lax.all_gather(cot, everyone, axis=0, tiled=True)
    all_fwd = lax.all_gather(x_fwd, everyone, axis=0, tiled=True)

    din_part = mm("tmd,dr->tmr", jnp.stack([x_fwd, x_bwd]), up_left[0])
    gdout_part = mm("md,rd->mr", cot, down_right[0])
    low_part = jnp.concatenate([din_part, gdout_part[None]]).astype(BF16)
    low = own_share(row_sum(low_part).astype(BF16), 2)
    low_all = lax.all_gather(low, everyone, axis=1, tiled=True)
    din_fwd, din_bwd, gdout = (per_section(low_all[i]) for i in range(3))

    right = lax.all_to_all(own_share(up_right[0], 0), "section", 1, 0, tiled=True)
    right = right.reshape(sections, share, units)
    left = lax.all_to_all(own_share(down_left[0], 0 + 1), "section", 0, 0, tiled=True)
    left = left.reshape(sections, units, share)

    def preact_of(tokens, din):
        part = mm("smd,df->smf", per_section(tokens), shared_up) + mm("smr,srf->smf", din, right)
        return row_sum(part.astype(BF16))

    pre_bwd = preact_of(all_bwd, din_bwd)
    ghid_part = mm("smd,fd->smf", per_section(all_cot), shared_down) + mm("smr,sfr->smf", gdout, left)
    grad_hidden = row_sum(ghid_part.astype(BF16))
    hid_bwd = jax.nn.silu(pre_bwd).astype(BF16)
    gpre = (grad_hidden * silu_slope(pre_bwd)).astype(BF16)
    flat_gpre = gpre.reshape(sections * micro, units)

    gnorm_part = mm("mf,df->md", flat_gpre, shared_up)
    gdin_part = mm("smf,srf->smr", gpre, right).reshape(sections * micro, share)
    back_part = jnp.concatenate([gnorm_part.astype(BF16), gdin_part.astype(BF16)], axis=1)
    back = lax.psum_scatter(back_part, everyone, scatter_dimension=0, tiled=True)
    gdin_own = row_gather(back[:, width:], 1)

    pre_fwd = preact_of(all_fwd, din_fwd)
    hid_fwd = jax.nn.silu(pre_fwd).astype(BF16)
    out_part = mm("mf,fd->md", hid_fwd.reshape(sections * micro, units), shared_down)
    dout_part = [
        mm("smf,sfr->smr", h, left).reshape(sections * micro, share).astype(BF16) for h in (hid_fwd, hid_bwd)
    ]
    ahead_part = jnp.concatenate([out_part.astype(BF16), *dout_part], axis=1)
    ahead = lax.psum_scatter(ahead_part, everyone, scatter_dimension=0, tiled=True)
    dout_own = row_gather(ahead[:, width:].reshape(own, 2, share), 2)

    grad_up = mm("md,mf->df", all_bwd, flat_gpre).astype(BF16)
    grad_down = mm("mf,md->fd", hid_bwd.reshape(sections * micro, units), all_cot).astype(BF16)

    grad_left = mm("smf,smr->sfr", hid_bwd, gdout).astype(BF16).reshape(sections * units, share)
    grad_left = lax.all_to_all(grad_left, "section", 0, 0, tiled=True)
    grad_down_left = row_gather(grad_left, 1).astype(F32)
    grad_right = mm("smr,smf->srf", din_bwd, gpre).astype(BF16).reshape(sections * share, units)
    grad_right = lax.all_to_all(grad_right, "section", 0, 1, tiled=True)
    grad_up_right = row_gather(grad_right, 0).astype(F32)

    grad_input = (
        cot.astype(F32) + back[:, :width].astype(F32) + mm("mr,dr->md", gdin_own, up_left[0])
    )
    handoff_bwd = from_behind(grad_input.astype(BF16)[None], "section", -1)
    gdin_all = lax.all_gather(gdin_own, "col", axis=0, tiled=True)
    grad_up_left = mm("md,mr->dr", own_section(all_bwd), gdin_all)

    out_fwd = (
        x_fwd.astype(F32) + ahead[:, :width].astype(F32) + mm("mr,rd->md", dout_own[:, 0], down_right[0])
    )
    handoff_fwd = from_behind(out_fwd.astype(BF16)[None], "section", 1)
    dout_all = lax.all_gather(dout_own[:, 1], "col", axis=0, tiled=True)
    grad_down_right = mm("mr,md->rd", dout_all, own_section(all_cot))
    return (
        handoff_fwd,
        handoff_bwd,
        grad_up,
        grad_down,
        grad_up_left[None],
        grad_up_right[None],
        grad_down_left[None],
        grad_down_right[None],
    )


def solution(mesh):
    in_specs = (
        P("section", "col", "row"),
        P("section", "col", "row"),
        P("section", "col", "row"),
        P("row", ("col", "section")),
        P(("col", "section"), "row"),
        P("section", "row", None),
        P("section", None, "col"),
        P("section", "col", None),
        P("section", None, "row"),
    )
    out_specs = (
        P("section", "col", "row"),
        P("section", "col", "row"),
        P("row", ("col", "section")),
        P(("col", "section"), "row"),
        P("section", "row", None),
        P("section", None, "col"),
        P("section", "col", None),
        P("section", None, "row"),
    )
    return jax.shard_map(local, mesh=mesh, in_specs=in_specs, out_specs=out_specs, check_vma=False)
```
